32 devices in a mesh: groups: 2 (over y), section: 4 (over x, core), dp: 4 (over z).
Axes of the slice: x: 2, y: 2, z: 4, core: 2. Of those that a mesh axis runs over, the one named last changes fastest.
Arguments:
- patches: bfloat16 [8192, 1024], P(('groups', 'dp'), 'section'), parts along dimension 0, may hold values from -6 to 6
- clip_slot: int32 [256], P('groups'), parts along dimension 0, may hold values from 0 to 127, each once
- w_qkv: bfloat16 [4, 1024, 1536], P('section'), may hold values from -0.1875 to 0.1875
- w_out: bfloat16 [4, 512, 1024], P('section'), may hold values from -0.25 to 0.25
- w_up: bfloat16 [4, 1024, 2048], P('section'), may hold values from -0.1875 to 0.1875
- w_down: bfloat16 [4, 2048, 1024], P('section'), may hold values from -0.125 to 0.125
- norm_gains: float32 [4, 2, 1024], P('section'), may hold values from 0.5 to 1.5
- level_one_weight: bfloat16 [3, 1024, 1024], P(None, 'section'), may hold values from -0.109375 to 0.109375
- level_two_weight: bfloat16 [3, 1024, 1024], P(None, 'section'), may hold values from -0.109375 to 0.109375
- head_weight: bfloat16 [1024, 22], P('section'), may hold values from -0.1875 to 0.1875
Outputs:
- level_one_heads: float32 [256, 22], P(('groups', 'dp')), parts along dimension 0
- level_two_heads: float32 [128, 22], P(('groups', 'dp')), parts along dimension 0
The draws below stay inside these ranges and needn't reach their ends.
There are 2 independent parts, one for each index of `groups`. The reference program is written for one: setup_inputs(seed, part) draws one part's arguments, and reference() takes and returns one part's arrays. A program takes and returns all parts, laid end to end along the dimension named above; an argument that names none is the same for every part. Nothing has to cross between parts.
Inputs may be any that keep to these rules, and one draw needn't show every extreme that they name: clip_slot is a permutation: every slot of the window holds exactly one clip.
All inputs are finite; a program needn't handle non-finite values.
Results may differ from the reference program's by a relative error of at most 0.035.
Values may be sent and summed in bfloat16 or wider, within the bound.
A program may use at most 64 MiB of HBM per device.

```python
import jax
import jax.numpy as jnp
from jax import lax

D = 1024
HEADS = 8
HEAD = 64
HID = 2048
HO = 22
PATCHES = 16
TUB_CLIP = 2
CLIP_TOK = 32
LAYERS = 4
N_CLIPS = 128


def levels(key, shape, split, low, largest):
    gain = 1.0
    for dim, blocks in split:
        draws = jax.random.uniform(jax.random.fold_in(jax.random.fold_in(key, 6), dim), (blocks,), jnp.float32, low / len(split), largest / len(split))
        gain = gain * jnp.repeat(jnp.exp(draws), shape[dim] // blocks).reshape((-1,) + (1,) * (len(shape) - 1 - dim))
    return gain


def noise(rng, extent, deviation, limit, cuts=(), kind=jnp.bfloat16):
    gain = levels(rng, extent, cuts, -0.22, 0.18) if cuts else 1.0
    array = jax.random.normal(rng, extent, jnp.float32) * deviation * gain
    return jnp.minimum(jnp.maximum(array, -limit), limit).astype(kind)


def setup_inputs(seed: int = 0, part: int = 0) -> dict:
    arg_keys = jax.random.split(jax.random.key(seed), 11)
    own_keys = jax.random.split(jax.random.fold_in(arg_keys[10], part), 11)
    return {
        "patches": noise(own_keys[0], (N_CLIPS * CLIP_TOK, D), 1.0, 6.0, ((0, 4), (1, 4))),
        "clip_slot": jax.random.permutation(own_keys[1], N_CLIPS).astype(jnp.int32),
        "w_qkv": noise(arg_keys[2], (LAYERS, D, 3 * HEADS * HEAD), D ** -0.5, 0.1875, ((0, 4),)),
        "w_out": noise(arg_keys[3], (LAYERS, HEADS * HEAD, D), (HEADS * HEAD) ** -0.5, 0.25, ((0, 4),)),
        "w_up": noise(arg_keys[4], (LAYERS, D, HID), D ** -0.5, 0.1875, ((0, 4),)),
        "w_down": noise(arg_keys[5], (LAYERS, HID, D), HID ** -0.5, 0.125, ((0, 4),)),
        "norm_gains": jnp.clip(1.0 + 0.1 * jax.random.normal(arg_keys[6], (LAYERS, 2, D), jnp.float32), 0.5, 1.5),
        "level_one_weight": noise(arg_keys[7], (3, D, D), (3 * D) ** -0.5, 0.109375, ((1, 4),)),
        "level_two_weight": noise(arg_keys[8], (3, D, D), (3 * D) ** -0.5, 0.109375, ((1, 4),)),
        "head_weight": noise(arg_keys[9], (D, HO), D ** -0.5, 0.1875, ((0, 4),)),
    }


EPSILON = 1e-05

def layer_norm(values, scaling):
    average = lax.optimization_barrier(jnp.mean(values, axis=-1, keepdims=True))
    centred = values - average
    spread = lax.optimization_barrier(jnp.mean(centred * centred, axis=-1, keepdims=True))
    return centred * lax.rsqrt(spread + EPSILON) * scaling

def head_norm(values):
    return values * lax.rsqrt(lax.optimization_barrier(jnp.mean(values * values, axis=-1, keepdims=True)) + EPSILON)

def vit_layer(stream, w_qkv, w_out, w_up, w_down, gains, clip_tok, head_count, head_size):
    row_count = stream.shape[0]
    clip_count = row_count // clip_tok
    residual = stream.astype(jnp.float32)
    normed = layer_norm(residual, gains[0]).astype(jnp.bfloat16)
    projected = jnp.dot(normed, w_qkv, preferred_element_type=jnp.float32)
    projected = projected.reshape(clip_count, clip_tok, 3, head_count, head_size)
    queries = head_norm(projected[:, :, 0]).astype(jnp.bfloat16)
    key_rows = head_norm(projected[:, :, 1]).astype(jnp.bfloat16)
    value_rows = projected[:, :, 2].astype(jnp.bfloat16)
    scores = jnp.einsum('cqhd,ckhd->chqk', queries.astype(jnp.float32), key_rows.astype(jnp.float32)) * head_size ** (-0.5)
    exponent = jnp.exp(scores)
    attention_weights = (exponent / lax.optimization_barrier(jnp.sum(exponent, axis=-1, keepdims=True))).astype(jnp.bfloat16)
    mixture = jnp.einsum('chqk,ckhd->cqhd', attention_weights.astype(jnp.float32), value_rows.astype(jnp.float32))
    mixture = mixture.astype(jnp.bfloat16).reshape(row_count, head_count * head_size)
    residual = residual + jnp.dot(mixture, w_out, preferred_element_type=jnp.float32)
    normed_b = layer_norm(residual, gains[1]).astype(jnp.bfloat16)
    hidden = jax.nn.gelu(jnp.dot(normed_b, w_up, preferred_element_type=jnp.float32), approximate=True).astype(jnp.bfloat16)
    residual = residual + jnp.dot(hidden, w_down, preferred_element_type=jnp.float32)
    return residual.astype(jnp.bfloat16)

def pyramid_level(inputs, weight):
    padded = jnp.concatenate([jnp.zeros((1, inputs.shape[1]), inputs.dtype), inputs], axis=0)
    length = inputs.shape[0]
    earlier_rows = padded[0:length:2]
    middle = padded[1:length + 1:2]
    later_rows = padded[2::2]
    summed = jnp.dot(earlier_rows, weight[0], preferred_element_type=jnp.float32)
    summed = summed + jnp.dot(middle, weight[1], preferred_element_type=jnp.float32)
    summed = summed + jnp.dot(later_rows, weight[2], preferred_element_type=jnp.float32)
    return jax.nn.gelu(summed, approximate=True).astype(jnp.bfloat16)

def reference(patches, clip_slot, w_qkv, w_out, w_up, w_down, norm_gains, level_one_weight, level_two_weight, head_weight):

    def advance(stream, layer_weights):
        return (vit_layer(stream, *layer_weights, CLIP_TOK, HEADS, HEAD), None)
    stream, _ = lax.scan(advance, patches, (w_qkv, w_out, w_up, w_down, norm_gains))
    tube_rows = stream.astype(jnp.float32).reshape(N_CLIPS * TUB_CLIP, PATCHES, D)
    pooled = lax.optimization_barrier(jnp.mean(tube_rows, axis=1)).astype(jnp.bfloat16)
    position = (clip_slot[:, None] * TUB_CLIP + jnp.arange(TUB_CLIP, dtype=jnp.int32)[None, :]).reshape(-1)
    film_rows = jnp.zeros_like(pooled).at[position].set(pooled)
    level_one = pyramid_level(film_rows, level_one_weight)
    level_two = pyramid_level(level_one, level_two_weight)
    level_one_heads = jnp.dot(level_one, head_weight, preferred_element_type=jnp.float32)
    level_two_heads = jnp.dot(level_two, head_weight, preferred_element_type=jnp.float32)
    return (level_one_heads, level_two_heads)
```

```python
import functools

import jax
import jax.numpy as jnp
from jax import lax
from jax.experimental import pallas as pl
from jax.experimental.pallas import tpu as pltpu
from jax.sharding import PartitionSpec as P

HEADS = 8
HEAD = 64
PATCHES = 16
TUB_CLIP = 2
EPSILON = 1e-05
UNIT_ROWS = 128
ROW_BLOCK = 128
CHUNK = 512
MESH = pl.DeviceIdType.MESH
F32 = jnp.float32
BF16 = jnp.bfloat16


def dot(a, b):
    return jnp.dot(a, b, preferred_element_type=F32)


def dot_nt(a, b):
    return lax.dot_general(a, b, (((1,), (1,)), ((), ())), preferred_element_type=F32)


def layer_norm(values, scaling):
    average = jnp.mean(values, axis=-1, keepdims=True)
    centred = values - average
    spread = jnp.mean(centred * centred, axis=-1, keepdims=True)
    return centred * lax.rsqrt(spread + EPSILON) * scaling


def gelu(values):
    return jax.nn.gelu(values, approximate=True)


def iota(shape, dim):
    return lax.broadcasted_iota(jnp.int32, shape, dim)


def head_scale(values):
    block = min(256, values.shape[1])
    same = iota((block, block), 0) // HEAD == iota((block, block), 1) // HEAD
    averaging = jnp.where(same, 1.0 / HEAD, 0.0).astype(BF16)
    squares = (values * values).astype(BF16)
    means = [
        dot(squares[:, start : start + block], averaging)
        for start in range(0, values.shape[1], block)
    ]
    return values * lax.rsqrt(jnp.concatenate(means, axis=1) + EPSILON)


def attention(queries, keys, values):
    clip = PATCHES * TUB_CLIP
    pair = 2 * HEAD
    rows = []
    cross = (2 * ROW_BLOCK, pair)
    own = (iota(cross, 0) < ROW_BLOCK) == (iota(cross, 1) < HEAD)
    own_bf = jnp.where(own, 1.0, 0.0).astype(BF16)
    square = (ROW_BLOCK, 2 * ROW_BLOCK)
    same_clip = iota(square, 0) // clip == (iota(square, 1) % ROW_BLOCK) // clip
    for start in range(0, queries.shape[0], ROW_BLOCK):
        mixed = []
        for lane in range(0, queries.shape[1], pair):
            q = queries[start : start + ROW_BLOCK, lane : lane + pair]
            k = keys[start : start + ROW_BLOCK, lane : lane + pair]
            v = values[start : start + ROW_BLOCK, lane : lane + pair]
            k2 = jnp.concatenate([k, k], axis=0) * own_bf
            v2 = jnp.concatenate([v, v], axis=0) * own_bf
            scores = dot_nt(q, k2)
            weights = jnp.where(same_clip, jnp.exp(scores), 0.0).astype(BF16)
            both = dot(weights, jnp.concatenate([v2, own_bf], axis=1))
            mixed.append((both[:, :pair] / both[:, pair:]).astype(BF16))
        rows.append(jnp.concatenate(mixed, axis=1))
    return jnp.concatenate(rows, axis=0) if len(rows) > 1 else rows[0]


def kernel(
    sections,
    shards,
    patches,
    clip_slot,
    w_qkv,
    w_out,
    w_up,
    w_down,
    gains,
    one_weight,
    two_weight,
    head_weight,
    head_one,
    head_two,
    v_qkv,
    v_out,
    v_up,
    v_down,
    v_one,
    v_two,
    gather,
    inbuf,
    outbuf,
    pooled_out,
    film_in,
    one_out,
    one_in,
    two_out,
    two_in,
    heads_out,
    heads_in,
    weight_sem,
    gather_send,
    gather_recv,
    hop_send,
    hop_recv,
    film_send,
    film_recv,
    ex_send,
    ex_recv,
):
    section = lax.axis_index("section")
    shard = lax.axis_index("dp")
    last = sections - 1
    units, unit_rows, width = inbuf.shape
    channels = width // sections
    tubes_unit = unit_rows // PATCHES
    hidden = v_up.shape[1]
    inner = v_out.shape[0]
    loads = [
        pltpu.make_async_copy(source, target, weight_sem.at[index])
        for index, (source, target) in enumerate(
            (
                (w_qkv.at[0], v_qkv),
                (w_out.at[0], v_out),
                (w_up.at[0], v_up),
                (w_down.at[0], v_down),
                (one_weight, v_one),
                (two_weight, v_two),
            )
        )
    ]
    for load in loads:
        load.start()

    barrier = pltpu.get_barrier_semaphore()
    for ds in range(sections):
        for dd in range(shards):
            if ds or dd:
                pl.semaphore_signal(
                    barrier,
                    inc=1,
                    device_id={
                        "section": lax.rem(section + ds, sections),
                        "dp": lax.rem(shard + dd, shards),
                    },
                    device_id_type=MESH,
                )
    pl.semaphore_wait(barrier, sections * shards - 1)

    def patch_rows(u):
        return pl.ds(pl.multiple_of(u * unit_rows, unit_rows), unit_rows)

    def patch_copy(u):
        return pltpu.make_async_remote_copy(
            src_ref=patches.at[patch_rows(u)],
            dst_ref=gather.at[section, u],
            send_sem=gather_send.at[u],
            recv_sem=gather_recv.at[section, u],
            device_id={"section": 0},
            device_id_type=MESH,
        )

    def patch_arrival(source, u):
        return pltpu.make_async_copy(
            patches.at[patch_rows(u)], gather.at[source, u], gather_recv.at[source, u]
        )

    def each_unit(body):
        def step(u, carry):
            body(u)
            return carry

        lax.fori_loop(0, units, step, 0)

    @pl.when(section > 0)
    def _():
        each_unit(lambda u: patch_copy(u).start())

    @pl.when(section == 0)
    def _():
        each_unit(lambda u: patch_arrival(0, u).start())

    def hop(u):
        return pltpu.make_async_remote_copy(
            src_ref=outbuf.at[u],
            dst_ref=inbuf.at[u],
            send_sem=hop_send.at[u],
            recv_sem=hop_recv.at[u],
            device_id={"section": lax.rem(section + 1, sections)},
            device_id_type=MESH,
        )

    def film_copy(u, target, step):
        return pltpu.make_async_remote_copy(
            src_ref=pooled_out.at[u, target],
            dst_ref=film_in.at[shard, u],
            send_sem=film_send.at[u, target, step],
            recv_sem=film_recv.at[shard, u],
            device_id={"section": target, "dp": lax.rem(shard + step, shards)},
            device_id_type=MESH,
        )

    film_targets = [
        (target, step)
        for target in range(sections)
        for step in range(shards)
        if not (target == last and step == 0)
    ]

    pooling_shape = (tubes_unit, unit_rows)
    pooling = jnp.where(
        iota(pooling_shape, 1) // PATCHES == iota(pooling_shape, 0), 1.0 / PATCHES, 0.0
    ).astype(BF16)

    def run_unit(u):
        @pl.when(section == 0)
        def _():
            for source in range(sections):
                patch_arrival(source, u).wait()
            inbuf[u] = jnp.concatenate([gather[source, u] for source in range(sections)], axis=1)

        @pl.when(section > 0)
        def _():
            hop(u).wait_recv()

        @pl.when(u == 0)
        def _():
            loads[0].wait()

        stream = inbuf[u].astype(F32)
        normed = layer_norm(stream, gains[0, 0:1]).astype(BF16)
        queries = (head_scale(dot(normed, v_qkv[:, :inner])) * HEAD**-0.5).astype(BF16)
        keys = head_scale(dot(normed, v_qkv[:, inner : 2 * inner])).astype(BF16)
        values = dot(normed, v_qkv[:, 2 * inner :]).astype(BF16)
        mixture = attention(queries, keys, values)

        @pl.when(u == 0)
        def _():
            loads[1].wait()
            loads[2].wait()
            loads[3].wait()

        residual = stream + dot(mixture, v_out[...])
        normed_b = layer_norm(residual, gains[0, 1:2]).astype(BF16)
        for start in range(0, hidden, CHUNK):
            part = gelu(dot(normed_b, v_up[:, start : start + CHUNK])).astype(BF16)
            residual = residual + dot(part, v_down[start : start + CHUNK, :])
        result = residual.astype(BF16)

        @pl.when(section < last)
        def _():
            outbuf[u] = result
            hop(u).start()

        @pl.when(section == last)
        def _():
            pooled = dot(pooling, result).astype(BF16).astype(F32)
            for target in range(sections):
                pooled_out[u, target] = pooled[:, target * channels : (target + 1) * channels]
            film_in[shard, u] = pooled[:, last * channels :]
            for target, step in film_targets:
                film_copy(u, target, step).start()

    each_unit(run_unit)

    loads[4].wait()
    loads[5].wait()

    def film_arrival(source, u):
        return pltpu.make_async_copy(
            film_in.at[source, u], film_in.at[source, u], film_recv.at[source, u]
        )

    @pl.when(section < last)
    def _():
        each_unit(lambda u: film_arrival(shard, u).wait())

    for step in range(1, shards):
        each_unit(lambda u: film_arrival(lax.rem(shard + step, shards), u).wait())

    tubes = shards * units * tubes_unit
    pooled = film_in[...].reshape(tubes, channels).astype(BF16)
    clips = tubes // TUB_CLIP
    spread_shape = (clips, tubes)
    spread = jnp.where(iota(spread_shape, 1) // TUB_CLIP == iota(spread_shape, 0), 1.0, 0.0)
    slots = jnp.broadcast_to(clip_slot[...].astype(F32), (8, clips)).astype(BF16)
    position = TUB_CLIP * dot(slots, spread.astype(BF16))[0:1]
    position = position + (iota((1, tubes), 1) % TUB_CLIP).astype(F32)

    two_rows = head_two.shape[0]
    one_rows = 3 * two_rows
    row = iota((one_rows, 1), 0)
    level_index = 2 * (shard * two_rows + row % two_rows) + row // two_rows - 1
    taps = []
    for tap in range(3):
        wanted = (2 * level_index + tap - 1).astype(F32)
        selector = jnp.where(position == wanted, 1.0, 0.0).astype(BF16)
        taps.append(dot(selector, pooled).astype(BF16))

    def conv(parts, weight):
        total = dot(parts[0], weight[0])
        for tap in (1, 2):
            total = total + dot(parts[tap], weight[tap])
        return total

    def exchange(stage, outgoing, incoming):
        copies = []
        for step in range(1, sections):
            target = lax.rem(section + step, sections)
            copies.append(
                pltpu.make_async_remote_copy(
                    src_ref=outgoing(target),
                    dst_ref=incoming.at[section],
                    send_sem=ex_send.at[stage, step],
                    recv_sem=ex_recv.at[stage, section],
                    device_id={"section": target},
                    device_id_type=MESH,
                )
            )
        for copy in copies:
            copy.start()

        def arrivals():
            for step in range(1, sections):
                source = lax.rem(section + step, sections)
                pltpu.make_async_copy(
                    incoming.at[source], incoming.at[source], ex_recv.at[stage, source]
                ).wait()
            for copy in copies:
                copy.wait_send()

        return arrivals

    def total(incoming):
        value = incoming[0].astype(F32)
        for source in range(1, sections):
            value = value + incoming[source].astype(F32)
        return value

    def scatter_sum(stage, partial, outgoing, incoming):
        partial = partial.astype(BF16)
        for target in range(sections):
            outgoing[target] = partial[:, target * channels : (target + 1) * channels]
        arrivals = exchange(stage, lambda target: outgoing.at[target], incoming)
        incoming[section] = outgoing[section]
        arrivals()
        return total(incoming)

    one = gelu(scatter_sum(0, conv(taps, v_one), one_out, one_in)).astype(BF16)
    parts = [one[block * two_rows : (block + 1) * two_rows] for block in range(3)]
    two_partial = conv(parts, v_two)
    two = gelu(scatter_sum(1, two_partial, two_out, two_in)).astype(BF16)

    natural = 2 * two_rows
    order = (natural, one_rows)
    chosen = iota(order, 1) == (1 + iota(order, 0) % 2) * two_rows + iota(order, 0) // 2
    one_natural = dot(jnp.where(chosen, 1.0, 0.0).astype(BF16), one).astype(BF16)
    outputs = head_weight.shape[1]
    heads_out[...] = jnp.zeros(heads_out.shape, F32)
    heads_out[0:natural, 0:outputs] = dot(one_natural, head_weight[...])
    heads_out[natural:, 0:outputs] = dot(two, head_weight[...])
    arrivals = exchange(2, lambda target: heads_out, heads_in)
    heads_in[section] = heads_out[...]
    arrivals()
    heads = total(heads_in)
    head_one[...] = heads[0:natural, 0:outputs]
    head_two[...] = heads[natural:, 0:outputs]

    @pl.when(section > 0)
    def _():
        each_unit(lambda u: patch_copy(u).wait_send())

    @pl.when(section < last)
    def _():
        each_unit(lambda u: hop(u).wait_send())

    @pl.when(section == last)
    def _():
        def finish(u):
            for target, step in film_targets:
                film_copy(u, target, step).wait_send()

        each_unit(finish)


def on_device(
    patches,
    clip_slot,
    w_qkv,
    w_out,
    w_up,
    w_down,
    norm_gains,
    level_one_weight,
    level_two_weight,
    head_weight,
):
    sections = lax.axis_size("section")
    shards = lax.axis_size("dp")
    rows, channels = patches.shape
    width = channels * sections
    unit_rows = UNIT_ROWS
    units = rows // unit_rows
    tubes_unit = unit_rows // PATCHES
    outputs = head_weight.shape[1]
    one_rows = rows // PATCHES // 2
    two_rows = one_rows // 2
    vmem = pl.BlockSpec(memory_space=pltpu.VMEM)
    anywhere = pl.BlockSpec(memory_space=pl.ANY)
    dma = pltpu.SemaphoreType.DMA
    return pl.pallas_call(
        functools.partial(kernel, sections, shards),
        out_shape=(
            jax.ShapeDtypeStruct((one_rows, outputs), F32),
            jax.ShapeDtypeStruct((two_rows, outputs), F32),
        ),
        in_specs=[anywhere, vmem] + [anywhere] * 4 + [vmem] + [anywhere] * 2 + [vmem],
        out_specs=(vmem, vmem),
        scratch_shapes=[
            pltpu.VMEM(w_qkv.shape[1:], BF16),
            pltpu.VMEM(w_out.shape[1:], BF16),
            pltpu.VMEM(w_up.shape[1:], BF16),
            pltpu.VMEM(w_down.shape[1:], BF16),
            pltpu.VMEM(level_one_weight.shape, BF16),
            pltpu.VMEM(level_two_weight.shape, BF16),
            pltpu.VMEM((sections, units, unit_rows, channels), BF16),
            pltpu.VMEM((units, unit_rows, width), BF16),
            pltpu.VMEM((units, unit_rows, width), BF16),
            pltpu.VMEM((units, sections, tubes_unit, channels), F32),
            pltpu.VMEM((shards, units, tubes_unit, channels), F32),
            pltpu.VMEM((sections, 3 * two_rows, channels), BF16),
            pltpu.VMEM((sections, 3 * two_rows, channels), BF16),
            pltpu.VMEM((sections, two_rows, channels), BF16),
            pltpu.VMEM((sections, two_rows, channels), BF16),
            pltpu.VMEM((3 * two_rows, 128), F32),
            pltpu.VMEM((sections, 3 * two_rows, 128), F32),
            dma((6,)),
            dma((units,)),
            dma((sections, units)),
            dma((units,)),
            dma((units,)),
            dma((units, sections, shards)),
            dma((shards, units)),
            dma((3, sections)),
            dma((3, sections)),
        ],
        compiler_params=pltpu.CompilerParams(
            collective_id=0, has_side_effects=True, vmem_limit_bytes=60 * 1024 * 1024
        ),
    )(
        patches,
        clip_slot.reshape(1, -1),
        w_qkv,
        w_out,
        w_up,
        w_down,
        norm_gains,
        level_one_weight,
        level_two_weight,
        head_weight,
    )


def solution(mesh):
    return jax.shard_map(
        on_device,
        mesh=mesh,
        in_specs=(
            P(("groups", "dp"), "section"),
            P("groups"),
            P("section", None, None),
            P("section", None, None),
            P("section", None, None),
            P("section", None, None),
            P("section", None, None),
            P(None, "section", None),
            P(None, "section", None),
            P("section", None),
        ),
        out_specs=(P(("groups", "dp"), None), P(("groups", "dp"), None)),
        check_vma=False,
    )
```

```python
import functools

import jax
import jax.numpy as jnp
from jax import lax
from jax.experimental import pallas as pl
from jax.experimental.pallas import tpu as pltpu
from jax.sharding import PartitionSpec as P

HEADS = 8
HEAD = 64
PATCHES = 16
TUB_CLIP = 2
EPSILON = 1e-05
UNIT_ROWS = 128
ROW_BLOCK = 128
CHUNK = 512
MESH = pl.DeviceIdType.MESH
F32 = jnp.float32
BF16 = jnp.bfloat16


def dot(a, b):
    return jnp.dot(a, b, preferred_element_type=F32)


def dot_nt(a, b):
    return lax.dot_general(a, b, (((1,), (1,)), ((), ())), preferred_element_type=F32)


def layer_norm(values, scaling):
    average = jnp.mean(values, axis=-1, keepdims=True)
    centred = values - average
    spread = jnp.mean(centred * centred, axis=-1, keepdims=True)
    return centred * lax.rsqrt(spread + EPSILON) * scaling


def gelu(values):
    return jax.nn.gelu(values, approximate=True)


def gelu_rounded(values):
    x = values.astype(BF16)
    inner = x * (x * x * 0.035677408136300125 + 0.7978845608028654)
    return x * (jnp.tanh(inner) * 0.5 + 0.5)


def iota(shape, dim):
    return lax.broadcasted_iota(jnp.int32, shape, dim)


def head_scale(values):
    block = min(256, values.shape[1])
    same = iota((block, block), 0) // HEAD == iota((block, block), 1) // HEAD
    averaging = jnp.where(same, 1.0 / HEAD, 0.0).astype(BF16)
    squares = (values * values).astype(BF16)
    means = [
        dot(squares[:, start : start + block], averaging)
        for start in range(0, values.shape[1], block)
    ]
    return values * lax.rsqrt(jnp.concatenate(means, axis=1) + EPSILON)


def attention(queries, keys, values):
    clip = PATCHES * TUB_CLIP
    pair = 2 * HEAD
    rows = []
    cross = (2 * ROW_BLOCK, pair)
    own = (iota(cross, 0) < ROW_BLOCK) == (iota(cross, 1) < HEAD)
    own_bf = jnp.where(own, 1.0, 0.0).astype(BF16)
    square = (ROW_BLOCK, 2 * ROW_BLOCK)
    same_clip = iota(square, 0) // clip == (iota(square, 1) % ROW_BLOCK) // clip
    for start in range(0, queries.shape[0], ROW_BLOCK):
        mixed = []
        for lane in range(0, queries.shape[1], pair):
            q = queries[start : start + ROW_BLOCK, lane : lane + pair]
            k = keys[start : start + ROW_BLOCK, lane : lane + pair]
            v = values[start : start + ROW_BLOCK, lane : lane + pair]
            k2 = jnp.concatenate([k, k], axis=0) * own_bf
            v2 = jnp.concatenate([v, v], axis=0) * own_bf
            scores = dot_nt(q, k2)
            weights = jnp.where(same_clip, jnp.exp(scores), 0.0).astype(BF16)
            both = dot(weights, jnp.concatenate([v2, own_bf], axis=1))
            mixed.append((both[:, :pair] / both[:, pair:]).astype(BF16))
        rows.append(jnp.concatenate(mixed, axis=1))
    return jnp.concatenate(rows, axis=0) if len(rows) > 1 else rows[0]


def kernel(
    sections,
    shards,
    patches,
    clip_slot,
    w_qkv,
    w_out,
    w_up,
    w_down,
    gains,
    one_weight,
    two_weight,
    head_weight,
    heads,
    v_qkv,
    v_out,
    v_up,
    v_down,
    v_one,
    v_two,
    gather,
    inbuf,
    outbuf,
    pooled_out,
    film_in,
    one_out,
    one_in,
    two_out,
    two_in,
    heads_out,
    heads_in,
    weight_sem,
    gather_send,
    gather_recv,
    hop_send,
    hop_recv,
    film_send,
    film_recv,
    ex_send,
    ex_recv,
):
    section = lax.axis_index("section")
    shard = lax.axis_index("dp")
    last = sections - 1
    units, unit_rows, width = inbuf.shape
    channels = width // sections
    tubes_unit = unit_rows // PATCHES
    hidden = v_up.shape[1]
    inner = v_out.shape[0]
    loads = [
        pltpu.make_async_copy(source, target, weight_sem.at[index])
        for index, (source, target) in enumerate(
            (
                (w_qkv.at[0], v_qkv),
                (w_out.at[0], v_out),
                (w_up.at[0], v_up),
                (w_down.at[0], v_down),
                (one_weight, v_one),
                (two_weight, v_two),
            )
        )
    ]
    for load in loads[:4]:
        load.start()

    barrier = pltpu.get_barrier_semaphore()
    for ds in range(sections):
        for dd in range(shards):
            if ds or dd:
                pl.semaphore_signal(
                    barrier,
                    inc=1,
                    device_id={
                        "section": lax.rem(section + ds, sections),
                        "dp": lax.rem(shard + dd, shards),
                    },
                    device_id_type=MESH,
                )
    pl.semaphore_wait(barrier, sections * shards - 1)

    def patch_rows(u):
        return pl.ds(pl.multiple_of(u * unit_rows, unit_rows), unit_rows)

    def patch_copy(u):
        return pltpu.make_async_remote_copy(
            src_ref=patches.at[patch_rows(u)],
            dst_ref=gather.at[section, u],
            send_sem=gather_send.at[u],
            recv_sem=gather_recv.at[section, u],
            device_id={"section": 0},
            device_id_type=MESH,
        )

    def patch_arrival(source, u):
        return pltpu.make_async_copy(
            patches.at[patch_rows(u)], gather.at[source, u], gather_recv.at[source, u]
        )

    def each_unit(body):
        def step(u, carry):
            body(u)
            return carry

        lax.fori_loop(0, units, step, 0)

    @pl.when(section > 0)
    def _():
        each_unit(lambda u: patch_copy(u).start())

    @pl.when(section == 0)
    def _():
        each_unit(lambda u: patch_arrival(0, u).start())

    def hop(u):
        return pltpu.make_async_remote_copy(
            src_ref=outbuf.at[u],
            dst_ref=inbuf.at[u],
            send_sem=hop_send.at[u],
            recv_sem=hop_recv.at[u],
            device_id={"section": lax.rem(section + 1, sections)},
            device_id_type=MESH,
        )

    def film_copy(u, target, step):
        return pltpu.make_async_remote_copy(
            src_ref=pooled_out.at[u, target],
            dst_ref=film_in.at[shard, u],
            send_sem=film_send.at[u, target, step],
            recv_sem=film_recv.at[shard, u],
            device_id={"section": target, "dp": lax.rem(shard + step, shards)},
            device_id_type=MESH,
        )

    film_targets = [
        (target, step)
        for target in range(sections)
        for step in range(shards)
        if not (target == last and step == 0)
    ]

    pooling_shape = (tubes_unit, unit_rows)
    pooling = jnp.where(
        iota(pooling_shape, 1) // PATCHES == iota(pooling_shape, 0), 1.0 / PATCHES, 0.0
    ).astype(BF16)

    def run_unit(u):
        @pl.when(section == 0)
        def _():
            for source in range(sections):
                patch_arrival(source, u).wait()
            inbuf[u] = jnp.concatenate([gather[source, u] for source in range(sections)], axis=1)

        @pl.when(section > 0)
        def _():
            hop(u).wait_recv()

        @pl.when(u == 0)
        def _():
            loads[0].wait()

        stream = inbuf[u].astype(F32)
        normed = layer_norm(stream, gains[0, 0:1]).astype(BF16)
        queries = (head_scale(dot(normed, v_qkv[:, :inner])) * HEAD**-0.5).astype(BF16)
        keys = head_scale(dot(normed, v_qkv[:, inner : 2 * inner])).astype(BF16)
        values = dot(normed, v_qkv[:, 2 * inner :]).astype(BF16)
        mixture = attention(queries, keys, values)

        @pl.when(u == 0)
        def _():
            for load in loads[1:4]:
                load.wait()
            for load in loads[4:]:
                load.start()

        residual = stream + dot(mixture, v_out[...])
        normed_b = layer_norm(residual, gains[0, 1:2]).astype(BF16)
        ahead = dot(normed_b, v_up[:, :CHUNK])
        for start in range(0, hidden, CHUNK):
            part = gelu_rounded(ahead)
            if start + CHUNK < hidden:
                ahead = dot(normed_b, v_up[:, start + CHUNK : start + 2 * CHUNK])
            residual = residual + dot(part, v_down[start : start + CHUNK, :])
        result = residual.astype(BF16)

        @pl.when(section < last)
        def _():
            outbuf[u] = result
            hop(u).start()

        @pl.when(section == last)
        def _():
            pooled = dot(pooling, result).astype(BF16).astype(F32)
            for target in range(sections):
                pooled_out[u, target] = pooled[:, target * channels : (target + 1) * channels]
            film_in[shard, u] = pooled[:, last * channels :]
            for target, step in film_targets:
                film_copy(u, target, step).start()

    each_unit(run_unit)

    loads[4].wait()
    loads[5].wait()

    def film_arrival(source, u):
        return pltpu.make_async_copy(
            film_in.at[source, u], film_in.at[source, u], film_recv.at[source, u]
        )

    @pl.when(section < last)
    def _():
        each_unit(lambda u: film_arrival(shard, u).wait())

    for step in range(1, shards):
        each_unit(lambda u: film_arrival(lax.rem(shard + step, shards), u).wait())

    tubes = shards * units * tubes_unit
    pooled = film_in[...].reshape(tubes, channels).astype(BF16)
    clips = tubes // TUB_CLIP
    spread_shape = (clips, tubes)
    spread = jnp.where(iota(spread_shape, 1) // TUB_CLIP == iota(spread_shape, 0), 1.0, 0.0)
    slots = jnp.broadcast_to(clip_slot[...].astype(F32), (8, clips)).astype(BF16)
    position = TUB_CLIP * dot(slots, spread.astype(BF16))[0:1]
    position = position + (iota((1, tubes), 1) % TUB_CLIP).astype(F32)

    two_rows = heads.shape[0] // 3
    one_rows = 3 * two_rows
    row = iota((one_rows, 1), 0)
    level_index = 2 * (shard * two_rows + row % two_rows) + row // two_rows - 1
    taps = []
    for tap in range(3):
        wanted = (2 * level_index + tap - 1).astype(F32)
        selector = jnp.where(position == wanted, 1.0, 0.0).astype(BF16)
        taps.append(dot(selector, pooled).astype(BF16))

    def conv(parts, weight):
        total = dot(parts[0], weight[0])
        for tap in (1, 2):
            total = total + dot(parts[tap], weight[tap])
        return total

    def exchange(stage, outgoing, incoming):
        copies = []
        for step in range(1, sections):
            target = lax.rem(section + step, sections)
            copies.append(
                pltpu.make_async_remote_copy(
                    src_ref=outgoing(target),
                    dst_ref=incoming.at[section],
                    send_sem=ex_send.at[stage, step],
                    recv_sem=ex_recv.at[stage, section],
                    device_id={"section": target},
                    device_id_type=MESH,
                )
            )
        for copy in copies:
            copy.start()

        def arrivals():
            for step in range(1, sections):
                source = lax.rem(section + step, sections)
                pltpu.make_async_copy(
                    incoming.at[source], incoming.at[source], ex_recv.at[stage, source]
                ).wait()
            for copy in copies:
                copy.wait_send()

        return arrivals

    def total(incoming):
        value = incoming[0].astype(F32)
        for source in range(1, sections):
            value = value + incoming[source].astype(F32)
        return value

    def scatter_sum(stage, partial, outgoing, incoming):
        partial = partial.astype(BF16)
        for target in range(sections):
            outgoing[target] = partial[:, target * channels : (target + 1) * channels]
        arrivals = exchange(stage, lambda target: outgoing.at[target], incoming)
        incoming[section] = outgoing[section]
        arrivals()
        return total(incoming)

    one = gelu(scatter_sum(0, conv(taps, v_one), one_out, one_in)).astype(BF16)
    parts = [one[block * two_rows : (block + 1) * two_rows] for block in range(3)]
    two_partial = conv(parts, v_two)
    two = gelu(scatter_sum(1, two_partial, two_out, two_in)).astype(BF16)

    natural = 2 * two_rows
    order = (natural, one_rows)
    chosen = iota(order, 1) == (1 + iota(order, 0) % 2) * two_rows + iota(order, 0) // 2
    one_natural = dot(jnp.where(chosen, 1.0, 0.0).astype(BF16), one).astype(BF16)
    outputs = head_weight.shape[0]
    heads_out[...] = jnp.zeros(heads_out.shape, F32)
    heads_out[0:natural, 0:outputs] = dot_nt(one_natural, head_weight[...])
    heads_out[natural:, 0:outputs] = dot_nt(two, head_weight[...])
    arrivals = exchange(2, lambda target: heads_out, heads_in)
    heads_in[section] = heads_out[...]
    arrivals()
    heads[...] = total(heads_in)

    @pl.when(section > 0)
    def _():
        each_unit(lambda u: patch_copy(u).wait_send())

    @pl.when(section < last)
    def _():
        each_unit(lambda u: hop(u).wait_send())

    @pl.when(section == last)
    def _():
        def finish(u):
            for target, step in film_targets:
                film_copy(u, target, step).wait_send()

        each_unit(finish)


def split_heads(heads, head_one, head_two):
    outputs, natural = head_one.shape
    head_one[...] = heads[0:natural].T[0:outputs]
    head_two[...] = heads[natural:, 0:outputs]


def on_device(
    patches,
    clip_slot,
    w_qkv,
    w_out,
    w_up,
    w_down,
    norm_gains,
    level_one_weight,
    level_two_weight,
    head_weight,
):
    sections = lax.axis_size("section")
    shards = lax.axis_size("dp")
    rows, channels = patches.shape
    width = channels * sections
    unit_rows = UNIT_ROWS
    units = rows // unit_rows
    tubes_unit = unit_rows // PATCHES
    outputs = head_weight.shape[1]
    one_rows = rows // PATCHES // 2
    two_rows = one_rows // 2
    vmem = pl.BlockSpec(memory_space=pltpu.VMEM)
    anywhere = pl.BlockSpec(memory_space=pl.ANY)
    dma = pltpu.SemaphoreType.DMA
    heads = pl.pallas_call(
        functools.partial(kernel, sections, shards),
        out_shape=jax.ShapeDtypeStruct((3 * two_rows, 128), F32),
        in_specs=[anywhere, vmem] + [anywhere] * 4 + [vmem] + [anywhere] * 2 + [vmem],
        out_specs=vmem,
        scratch_shapes=[
            pltpu.VMEM(w_qkv.shape[1:], BF16),
            pltpu.VMEM(w_out.shape[1:], BF16),
            pltpu.VMEM(w_up.shape[1:], BF16),
            pltpu.VMEM(w_down.shape[1:], BF16),
            pltpu.VMEM(level_one_weight.shape, BF16),
            pltpu.VMEM(level_two_weight.shape, BF16),
            pltpu.VMEM((sections, units, unit_rows, channels), BF16),
            pltpu.VMEM((units, unit_rows, width), BF16),
            pltpu.VMEM((units, unit_rows, width), BF16),
            pltpu.VMEM((units, sections, tubes_unit, channels), F32),
            pltpu.VMEM((shards, units, tubes_unit, channels), F32),
            pltpu.VMEM((sections, 3 * two_rows, channels), BF16),
            pltpu.VMEM((sections, 3 * two_rows, channels), BF16),
            pltpu.VMEM((sections, two_rows, channels), BF16),
            pltpu.VMEM((sections, two_rows, channels), BF16),
            pltpu.VMEM((3 * two_rows, 128), F32),
            pltpu.VMEM((sections, 3 * two_rows, 128), F32),
            dma((6,)),
            dma((units,)),
            dma((sections, units)),
            dma((units,)),
            dma((units,)),
            dma((units, sections, shards)),
            dma((shards, units)),
            dma((3, sections)),
            dma((3, sections)),
        ],
        compiler_params=pltpu.CompilerParams(
            collective_id=0, has_side_effects=True, vmem_limit_bytes=60 * 1024 * 1024
        ),
    )(
        patches,
        clip_slot.reshape(1, -1),
        w_qkv,
        w_out,
        w_up,
        w_down,
        norm_gains,
        level_one_weight,
        level_two_weight,
        head_weight.T,
    )
    head_one, head_two = pl.pallas_call(
        split_heads,
        out_shape=(
            jax.ShapeDtypeStruct((outputs, one_rows), F32),
            jax.ShapeDtypeStruct((two_rows, outputs), F32),
        ),
        in_specs=[vmem],
        out_specs=(vmem, vmem),
    )(heads)
    return head_one.T, head_two


def solution(mesh):
    return jax.shard_map(
        on_device,
        mesh=mesh,
        in_specs=(
            P(("groups", "dp"), "section"),
            P("groups"),
            P("section", None, None),
            P("section", None, None),
            P("section", None, None),
            P("section", None, None),
            P("section", None, None),
            P(None, "section", None),
            P(None, "section", None),
            P("section", None),
        ),
        out_specs=(P(("groups", "dp"), None), P(("groups", "dp"), None)),
        check_vma=False,
    )
```
